512 devices in a mesh: cache: 64 (over x, z, core), rank: 8 (over y).
Axes of the slice: x: 4, y: 8, z: 8, core: 2. Of those that a mesh axis runs over, the one named last changes fastest.
Arguments:
- cand_rows: bfloat16 [64, 64, 4, 1024], P('cache', None, None, 'rank'), may hold values from -48 to 48
- listed: int32 [64], replicated, may hold values from 0 to 63, each once
- hist_len: int32 [64], P('cache'), may hold values from 768 to 3072, as said below
- block_mask: int32 [64, 24], P('cache'), may hold values 0 or 1
- hist_keys: bfloat16 [1, 64, 3072, 1024], P(None, 'cache', None, 'rank'), may hold values from -6 to 6
- hist_values: bfloat16 [1, 64, 3072, 1024], P(None, 'cache', None, 'rank'), may hold values from -6 to 6
- w_query: bfloat16 [1, 1024, 1024], P(None, None, 'rank'), may hold values from -0.1875 to 0.1875
- w_gate: bfloat16 [1, 1024, 1024], P(None, None, 'rank'), may hold values from -0.1875 to 0.1875
- w_out: bfloat16 [1, 1024, 1024], P(None, None, 'rank'), may hold values from -0.1875 to 0.1875
Outputs:
- ranked: bfloat16 [64, 64, 4, 1024], P('cache', None, None, 'rank')
The draws below stay inside these ranges and needn't reach their ends.
Inputs may be any that keep to these rules, and one draw needn't show every extreme that they name: `hist_len`: some user has exactly 3072 history events. `listed`: each user id appears once.
All inputs are finite; a program needn't handle non-finite values. No bound on the sum of `block_mask` on one device may be relied on, other than what follows from the above.
Results may differ from the reference program's by a relative error of at most 0.0024.
Values may be sent and summed in bfloat16 or wider, within the bound.
A program may use at most 64 MiB of HBM per device.

```python
import math
import jax
import jax.numpy as jnp
from jax import lax

D = 1024
HEADS = 8
BLOCK = 128
NB = 24
HIST = 3072
CPR = 4
SHARDS = 64
USERS = 64
LAYERS = 1


def draw_cand_rows(key, part):
    first_key = jax.random.fold_in(key, 11)
    second_key = jax.random.fold_in(key, 12)
    row_scale = jnp.exp(jax.random.uniform(second_key, (SHARDS, USERS, CPR, 1), jnp.float32, 0.0, math.log(10.0)))
    base_vals = jnp.clip(jax.random.normal(first_key, (SHARDS, USERS, CPR, D), jnp.float32), -4.0, 4.0)
    return (base_vals * row_scale).astype(jnp.bfloat16)


def draw_hist_len(key, part):
    first_key = jax.random.fold_in(key, 21)
    second_key = jax.random.fold_in(key, 22)
    lengths = jax.random.randint(first_key, (USERS,), NB * BLOCK // 4, NB * BLOCK + 1, jnp.int32)
    longest = jax.random.randint(second_key, (), 0, USERS, jnp.int32)
    return lengths.at[longest].set(NB * BLOCK)


def with_ends(entries, stream_key, low, top_value):
    longest = entries.shape.index(max(entries.shape))
    spots = []
    for shift in (0, 1):
        where = [jax.random.randint(jax.random.fold_in(stream_key, axis), (), 0, length) for axis, length in enumerate(entries.shape)]
        where[longest] = (where[longest] + shift) % entries.shape[longest]
        spots.append(tuple(where))
    return entries.at[spots[0]].set(low).at[spots[1]].set(top_value)


def block_scale(stream_key, extent, cuts, smallest, largest):
    gain = 1.0
    for axis_at, shards_of in cuts:
        heights = jax.random.uniform(jax.random.fold_in(jax.random.fold_in(stream_key, 6), axis_at), (shards_of,), jnp.float32, smallest / len(cuts), largest / len(cuts))
        gain = gain * jnp.repeat(jnp.exp(heights), extent[axis_at] // shards_of).reshape((-1,) + (1,) * (len(extent) - 1 - axis_at))
    return gain


def bell_draw(rng, shape, deviation, bound, shards=(), kind=jnp.bfloat16):
    entries = jax.random.normal(rng, shape, jnp.float32) * deviation
    if len(shards) > 0:
        entries = block_scale(rng, shape, shards, -0.22, 0.18) * entries
    return jnp.clip(entries, min=-bound, max=bound).astype(kind)


def setup_inputs(seed: int = 0) -> dict:
    seeds = jax.random.split(jax.random.key(seed), 10)
    cand_rows = draw_cand_rows(jax.random.fold_in(seeds[9], 71), 0)
    listed = jax.random.permutation(seeds[1], USERS).astype(jnp.int32)
    hist_len = draw_hist_len(jax.random.fold_in(seeds[9], 71), 0)
    block_mask = with_ends((jax.random.randint(seeds[3], (USERS, NB), 0, 4) < 3).astype(jnp.int32), jax.random.fold_in(seeds[3], 1), 0, 1)
    hist_keys = bell_draw(seeds[4], (LAYERS, USERS, HIST, D), 1.0, 6.0, ((1, 64), (3, 8)))
    hist_values = bell_draw(seeds[5], (LAYERS, USERS, HIST, D), 1.0, 6.0, ((1, 64), (3, 8)))
    w_query = bell_draw(seeds[6], (LAYERS, D, D), D ** -0.5, 0.1875, ((2, 8),))
    w_gate = bell_draw(seeds[7], (LAYERS, D, D), D ** -0.5, 0.1875, ((2, 8),))
    w_out = bell_draw(seeds[8], (LAYERS, D, D), D ** -0.5, 0.1875, ((2, 8),))
    return dict(cand_rows=cand_rows, listed=listed, hist_len=hist_len, block_mask=block_mask, hist_keys=hist_keys, hist_values=hist_values, w_query=w_query, w_gate=w_gate, w_out=w_out)


EPSILON = 1e-05

def head_norm(values):
    centre = lax.optimization_barrier(jnp.mean(values, axis=-1, keepdims=True))
    spread = lax.optimization_barrier(jnp.mean(jnp.square(values - centre), axis=-1, keepdims=True))
    return (values - centre) * lax.rsqrt(spread + EPSILON)

def reference(cand_rows, listed, hist_len, block_mask, hist_keys, hist_values, w_query, w_gate, w_out):
    head_size = D // HEADS
    positions = jnp.arange(NB * BLOCK, dtype=jnp.int32)

    def one_slot(slot_no):
        user_id = listed[slot_no]
        cand_feats = lax.dynamic_index_in_dim(cand_rows, slot_no, 1, keepdims=False).reshape(SHARDS * CPR, D)
        user_blocks = lax.dynamic_index_in_dim(block_mask, user_id, 0, keepdims=False)
        length = lax.dynamic_index_in_dim(hist_len, user_id, 0, keepdims=False)
        live_mask = ((positions < length) & (user_blocks[positions // BLOCK] == 1)).astype(jnp.float32)
        for layer_no in range(LAYERS):
            key_cache = lax.dynamic_index_in_dim(hist_keys[layer_no], user_id, 0, keepdims=False)
            value_cache = lax.dynamic_index_in_dim(hist_values[layer_no], user_id, 0, keepdims=False)
            key_cache = key_cache.reshape(NB * BLOCK, HEADS, head_size).astype(jnp.float32)
            value_cache = value_cache.reshape(NB * BLOCK, HEADS, head_size).astype(jnp.float32)
            normed = head_norm(cand_feats.astype(jnp.float32)).astype(jnp.bfloat16)
            queries = jax.nn.silu(jnp.dot(normed, w_query[layer_no], preferred_element_type=jnp.float32)).astype(jnp.bfloat16)
            gate_act = jax.nn.silu(jnp.dot(normed, w_gate[layer_no], preferred_element_type=jnp.float32))
            query_heads = queries.reshape(SHARDS * CPR, HEADS, head_size).astype(jnp.float32)
            scores = jnp.einsum('che,the->cht', query_heads, key_cache) * head_size ** (-0.5)
            weights = (jax.nn.silu(scores) * live_mask[None, None, :]).astype(jnp.bfloat16)
            weights = lax.optimization_barrier(weights).astype(jnp.float32)
            attended = jnp.einsum('cht,the->che', weights, value_cache)
            hidden = head_norm(attended) * gate_act.reshape(SHARDS * CPR, HEADS, head_size)
            hidden = hidden.reshape(SHARDS * CPR, D).astype(jnp.bfloat16)
            projected = jnp.dot(hidden, w_out[layer_no], preferred_element_type=jnp.float32)
            cand_feats = (cand_feats.astype(jnp.float32) + projected).astype(jnp.bfloat16)
        return cand_feats.reshape(SHARDS, CPR, D)
    outputs = lax.map(one_slot, jnp.arange(USERS, dtype=jnp.int32))
    return jnp.transpose(outputs, (1, 0, 2, 3))
```

```python
import functools

import jax
import jax.numpy as jnp
from jax import lax
from jax.experimental import pallas as pl
from jax.experimental.pallas import tpu as pltpu
from jax.sharding import PartitionSpec as P

BLOCK = 128
EPSILON = 1e-05
CHUNKS = 2
KEY_TILE = 512
F32 = jnp.float32
BF16 = jnp.bfloat16


def silu(values):
    half = values * 0.5
    return half + half * jnp.tanh(half)


def layer_kernel(
    caches, ranks, cpr,
    cand, listed, hist_len, block_mask, keys, values, w_query, w_gate, w_out,
    ranked,
    cand_v, listed_v, length_s, mask_s, keys_v, values_v, w_in_v, w_out_v, place, send1, gathered, hidden, send2, recv2,
    load_sem, a_send, a_recv, ring_send, ring_recv, b_send, b_recv,
):
    my_cache = lax.axis_index("cache")
    my_rank = lax.axis_index("rank")
    rows = caches * cpr
    part = rows // CHUNKS
    head = keys.shape[1]
    hist = keys.shape[0]
    right = lax.rem(my_rank + 1, ranks)
    left = lax.rem(my_rank + ranks - 1, ranks)

    loads = [
        pltpu.make_async_copy(cand, cand_v, load_sem.at[0]),
        pltpu.make_async_copy(w_query, w_in_v.at[:, pl.ds(0, head)], load_sem.at[1]),
        pltpu.make_async_copy(w_gate, w_in_v.at[:, pl.ds(head, head)], load_sem.at[2]),
        pltpu.make_async_copy(values, values_v, load_sem.at[3]),
        pltpu.make_async_copy(keys, keys_v, load_sem.at[4]),
        pltpu.make_async_copy(w_out, w_out_v, load_sem.at[5]),
        pltpu.make_async_copy(listed, listed_v, load_sem.at[6]),
        pltpu.make_async_copy(hist_len, length_s, load_sem.at[7]),
        pltpu.make_async_copy(block_mask, mask_s, load_sem.at[8]),
    ]
    for load in loads:
        load.start()

    barrier = pltpu.get_barrier_semaphore()

    def greet(step, carry):
        peer = lax.rem(my_cache + step, caches)
        pl.semaphore_signal(barrier, inc=1, device_id={"cache": peer}, device_id_type=pl.DeviceIdType.MESH)
        return carry

    lax.fori_loop(1, caches, greet, 0)
    for peer in (left, right):
        pl.semaphore_signal(barrier, inc=1, device_id={"rank": peer}, device_id_type=pl.DeviceIdType.MESH)

    users = caches
    slot_of = (
        lax.broadcasted_iota(jnp.int32, (users, rows), 1) // cpr
        == lax.broadcasted_iota(jnp.int32, (users, rows), 0)
    ).astype(F32).astype(BF16)
    loads[6].wait()
    listed_rows = jnp.broadcast_to(listed_v[...].astype(F32), (8, users)).astype(BF16)
    user_of = jnp.dot(listed_rows, slot_of, preferred_element_type=F32)[0:1, :]
    column = lax.broadcasted_iota(jnp.int32, (1, rows), 1)
    target = user_of * cpr + lax.rem(column, cpr).astype(F32)
    row_no = lax.broadcasted_iota(jnp.int32, (rows, rows), 0).astype(F32)
    moved = jnp.where(row_no == target, 1.0, 0.0)
    place[...] = moved.T.astype(BF16)
    loads[0].wait()
    send1[...] = jnp.dot(
        moved.astype(BF16), cand_v[...], preferred_element_type=F32
    ).astype(BF16)

    pl.semaphore_wait(barrier, caches - 1 + 2)

    def send_user(step, carry):
        peer = lax.rem(my_cache + step, caches)
        pltpu.make_async_remote_copy(
            src_ref=send1.at[pl.ds(pl.multiple_of(peer * cpr, cpr), cpr)],
            dst_ref=gathered.at[my_rank, pl.ds(pl.multiple_of(my_cache * cpr, cpr), cpr)],
            send_sem=a_send,
            recv_sem=a_recv,
            device_id={"cache": peer},
            device_id_type=pl.DeviceIdType.MESH,
        ).start()
        return carry

    lax.fori_loop(1, caches, send_user, 0)
    mine = pl.ds(pl.multiple_of(my_cache * cpr, cpr), cpr)
    pltpu.make_async_copy(send1.at[mine], gathered.at[my_rank, mine], a_recv).start()

    loads[3].wait()
    loads[7].wait()
    loads[8].wait()
    length = length_s[0]
    for block in range(hist // BLOCK):
        events = pl.ds(block * BLOCK, BLOCK)
        limit = (length - block * BLOCK) * (mask_s[0, block] == 1).astype(jnp.int32)
        live = (lax.broadcasted_iota(jnp.int32, (BLOCK, head), 0) < limit).astype(F32)
        values_v[events, :] = (values_v[events, :].astype(F32) * live).astype(BF16)

    for load in (loads[1], loads[2], loads[4], loads[5]):
        load.wait()
    pltpu.make_async_copy(gathered.at[my_rank], gathered.at[my_rank], a_recv).wait()

    def ring_copy(buffer, phase, chunk, way, step):
        owner = lax.rem(my_rank + (ranks - step if way == 0 else step), ranks)
        span = pl.ds(chunk * part, part)
        return pltpu.make_async_remote_copy(
            src_ref=buffer.at[owner, span],
            dst_ref=buffer.at[owner, span],
            send_sem=ring_send.at[phase, chunk, way, step],
            recv_sem=ring_recv.at[phase, chunk, way, step],
            device_id={"rank": right if way == 0 else left},
            device_id_type=pl.DeviceIdType.MESH,
        )

    half = ranks // 2

    def steps_of(chunk, way):
        return half if (chunk % 2 == 0) == (way == 0) else half - 1

    def ring_wait(buffer, phase, chunk, way, step):
        ring_copy(buffer, phase, chunk, way, step).wait_recv()

    def ring_forward(buffer, phase, chunk, step):
        for way in (0, 1):
            if step > 0 and step - 1 < steps_of(chunk, way):
                ring_wait(buffer, phase, chunk, way, step - 1)
            if step < steps_of(chunk, way):
                ring_copy(buffer, phase, chunk, way, step).start()

    for step in range(half):
        for chunk in range(CHUNKS):
            ring_forward(gathered, 0, chunk, step)

    for chunk in range(CHUNKS):
        ring_forward(gathered, 0, chunk, half)
        span = pl.ds(chunk * part, part)
        slices = [gathered[k, span, :].astype(F32) for k in range(ranks)]
        centre = jnp.sum(sum(slices[1:], slices[0]), axis=-1, keepdims=True) * (1.0 / (ranks * head))
        slices = [s - centre for s in slices]
        squares = [s * s for s in slices]
        spread = jnp.sum(sum(squares[1:], squares[0]), axis=-1, keepdims=True) * (1.0 / (ranks * head))
        factor = lax.rsqrt(spread + EPSILON)
        normed = jnp.concatenate([(s * factor).astype(BF16) for s in slices], axis=1)
        both = silu(jnp.dot(normed, w_in_v[...], preferred_element_type=F32))
        queries = both[:, :head].astype(BF16)
        gate = both[:, head:]
        attended = jnp.zeros((part, head), F32)
        for tile in range(hist // KEY_TILE):
            events = pl.ds(tile * KEY_TILE, KEY_TILE)
            scores = lax.dot_general(
                queries, keys_v[events, :], (((1,), (1,)), ((), ())), preferred_element_type=F32
            )
            weights = silu(scores * (head ** -0.5)).astype(BF16)
            attended += jnp.dot(weights, values_v[events, :], preferred_element_type=F32)
        centre = jnp.mean(attended, axis=-1, keepdims=True)
        attended = attended - centre
        spread = jnp.mean(attended * attended, axis=-1, keepdims=True)
        hidden[my_rank, span, :] = (attended * lax.rsqrt(spread + EPSILON) * gate).astype(BF16)
        ring_forward(hidden, 1, chunk, 0)

    for step in range(1, half):
        for chunk in range(CHUNKS):
            ring_forward(hidden, 1, chunk, step)

    shards = caches // CHUNKS
    for chunk in range(CHUNKS):
        ring_forward(hidden, 1, chunk, half)
        span = pl.ds(chunk * part, part)
        whole = jnp.concatenate([hidden[k, span, :] for k in range(ranks)], axis=1)
        projected = jnp.dot(whole, w_out_v[...], preferred_element_type=F32)
        send2[span, :] = (gathered[my_rank, span, :].astype(F32) + projected).astype(BF16)

        def send_shard(step, carry, chunk=chunk):
            peer = chunk * shards + lax.rem(my_cache + step, shards)
            there = pl.ds(pl.multiple_of(peer * cpr, cpr), cpr)

            @pl.when(peer != my_cache)
            def _():
                pltpu.make_async_remote_copy(
                    src_ref=send2.at[there],
                    dst_ref=recv2.at[mine],
                    send_sem=b_send,
                    recv_sem=b_recv,
                    device_id={"cache": peer},
                    device_id_type=pl.DeviceIdType.MESH,
                ).start()

            @pl.when(peer == my_cache)
            def _():
                pltpu.make_async_copy(send2.at[mine], recv2.at[mine], b_recv).start()

            return carry

        lax.fori_loop(0, shards, send_shard, 0)

    pltpu.make_async_copy(recv2, recv2, b_recv).wait()
    ranked[...] = jnp.dot(place[...], recv2[...], preferred_element_type=F32).astype(BF16)

    others = pl.ds(0, rows - cpr)
    pltpu.make_async_copy(send1.at[others], send1.at[others], a_send).wait()
    pltpu.make_async_copy(send2.at[others], send2.at[others], b_send).wait()
    for phase, buffer in ((0, gathered), (1, hidden)):
        for chunk in range(CHUNKS):
            for way in (0, 1):
                for step in range(steps_of(chunk, way)):
                    ring_copy(buffer, phase, chunk, way, step).wait_send()


def on_device(
    cand_rows, listed, hist_len, block_mask, hist_keys, hist_values, w_query, w_gate, w_out, *, caches, ranks
):
    _, users, cpr, width = cand_rows.shape
    rows = users * cpr
    hist = hist_keys.shape[2]
    depth = w_query.shape[1]
    in_hbm = pl.BlockSpec(memory_space=pltpu.HBM)
    vmem = pl.BlockSpec(memory_space=pltpu.VMEM)
    half = ranks // 2
    ranked = pl.pallas_call(
        functools.partial(layer_kernel, caches, ranks, cpr),
        out_shape=jax.ShapeDtypeStruct((rows, width), BF16),
        in_specs=[in_hbm] * 9,
        out_specs=vmem,
        scratch_shapes=[
            pltpu.VMEM((rows, width), BF16),
            pltpu.VMEM((1, users), jnp.int32),
            pltpu.SMEM(hist_len.shape, jnp.int32),
            pltpu.SMEM(block_mask.shape, jnp.int32),
            pltpu.VMEM((hist, width), BF16),
            pltpu.VMEM((hist, width), BF16),
            pltpu.VMEM((depth, 2 * width), BF16),
            pltpu.VMEM((depth, width), BF16),
            pltpu.VMEM((rows, rows), BF16),
            pltpu.VMEM((rows, width), BF16),
            pltpu.VMEM((ranks, rows, width), BF16),
            pltpu.VMEM((ranks, rows, width), BF16),
            pltpu.VMEM((rows, width), BF16),
            pltpu.VMEM((rows, width), BF16),
            pltpu.SemaphoreType.DMA((9,)),
            pltpu.SemaphoreType.DMA,
            pltpu.SemaphoreType.DMA,
            pltpu.SemaphoreType.DMA((2, CHUNKS, 2, half)),
            pltpu.SemaphoreType.DMA((2, CHUNKS, 2, half)),
            pltpu.SemaphoreType.DMA,
            pltpu.SemaphoreType.DMA,
        ],
        compiler_params=pltpu.CompilerParams(
            collective_id=0, has_side_effects=True, vmem_limit_bytes=56 * 1024 * 1024
        ),
        name="hstu_layer",
    )(
        cand_rows.reshape(rows, width),
        listed.reshape(1, users),
        hist_len,
        block_mask,
        hist_keys.reshape(hist, width),
        hist_values.reshape(hist, width),
        w_query.reshape(depth, width),
        w_gate.reshape(depth, width),
        w_out.reshape(depth, width),
    )
    return ranked.reshape(cand_rows.shape)


def solution(mesh):
    placed = (
        P("cache", None, None, "rank"),
        P(),
        P("cache"),
        P("cache", None),
        P(None, "cache", None, "rank"),
        P(None, "cache", None, "rank"),
        P(None, None, "rank"),
        P(None, None, "rank"),
        P(None, None, "rank"),
    )
    return jax.shard_map(
        functools.partial(on_device, caches=mesh.shape["cache"], ranks=mesh.shape["rank"]),
        mesh=mesh,
        in_specs=placed,
        out_specs=P("cache", None, None, "rank"),
        check_vma=False,
    )
```

```python
import functools

import jax
import jax.numpy as jnp
from jax import lax
from jax.experimental import pallas as pl
from jax.experimental.pallas import tpu as pltpu
from jax.sharding import PartitionSpec as P

BLOCK = 128
EPSILON = 1e-05
CHUNKS = 2
KEY_TILE = 512
F32 = jnp.float32
BF16 = jnp.bfloat16


def silu(values):
    half = values * 0.5
    return half + half * jnp.tanh(half)


DEPTHS = 8
MESH = pl.DeviceIdType.MESH
FAR_X = (2, 1, 3, 0)


def layer_kernel(
    caches, ranks, cpr,
    cand, listed, hist_len, block_mask, keys, values, w_query, w_gate, w_out,
    ranked,
    cand_v, listed_v, length_s, mask_s, keys_v, values_v, w_in_v, w_out_v, place, send1, gathered, hidden,
    send2, recv2, load_sem, a_send, a_recv, near_recv, rest_recv, ring_send, b_send, b_recv,
):
    my_cache = lax.axis_index("cache")
    my_rank = lax.axis_index("rank")
    rows = caches * cpr
    part = rows // CHUNKS
    head = keys.shape[1]
    hist = keys.shape[0]
    wide = caches // (2 * DEPTHS)
    my_core = lax.rem(my_cache, 2)
    my_z = lax.rem(my_cache // 2, DEPTHS)
    my_x = my_cache // (2 * DEPTHS)

    barrier = pltpu.get_barrier_semaphore()

    def peer_at(dx, dz, dc):
        x, z, core = lax.rem(my_x + dx, wide), lax.rem(my_z + dz, DEPTHS), lax.rem(my_core + dc, 2)
        return (x * DEPTHS + z) * 2 + core

    def back(step, extent):
        return (extent - step) % extent if isinstance(step, int) else lax.rem(extent - step, extent)

    def for_depths(places, body):
        def one(step, carry):
            away = (step + 1) // 2
            dz = lax.rem(DEPTHS + DEPTHS // 2 + away * (1 - 2 * lax.rem(step, 2)), DEPTHS)
            for dx in places:
                for dc in (0, 1):
                    body(dx, dz, dc)
            return carry

        lax.fori_loop(0, DEPTHS - 1, one, 0)
        for dx in places:
            for dc in (0, 1):
                if (dx, dc) != (0, 0):
                    body(dx, 0, dc)

    def greet(dx, dz, dc):
        pl.semaphore_signal(
            barrier, inc=1, device_id={"cache": peer_at(dx, dz, dc)}, device_id_type=MESH
        )

    for_depths(FAR_X, greet)

    def rank_at(step):
        return lax.rem(my_rank + (step + ranks), ranks)

    for step in (-2, -1, 1, 2):
        pl.semaphore_signal(barrier, inc=1, device_id={"rank": rank_at(step)}, device_id_type=MESH)

    def load(source, target, number):
        return pltpu.make_async_copy(source, target, load_sem.at[number])

    loads = [
        load(cand, cand_v, 0),
        load(listed, listed_v, 1),
        load(values, values_v, 2),
        load(hist_len, length_s, 3),
        load(block_mask, mask_s, 4),
        load(keys, keys_v, 5),
        load(w_query, w_in_v.at[:, pl.ds(0, head)], 6),
        load(w_gate, w_in_v.at[:, pl.ds(head, head)], 7),
        load(w_out, w_out_v, 8),
    ]
    for one in loads:
        one.start()

    users = caches
    slot_of = (
        lax.broadcasted_iota(jnp.int32, (users, rows), 1) // cpr
        == lax.broadcasted_iota(jnp.int32, (users, rows), 0)
    ).astype(F32).astype(BF16)
    loads[1].wait()
    listed_rows = jnp.broadcast_to(listed_v[...].astype(F32), (8, users)).astype(BF16)
    user_of = jnp.dot(listed_rows, slot_of, preferred_element_type=F32)[0:1, :]
    column = lax.broadcasted_iota(jnp.int32, (1, rows), 1)
    target = user_of * cpr + lax.rem(column, cpr).astype(F32)
    row_no = lax.broadcasted_iota(jnp.int32, (rows, rows), 0).astype(F32)
    moved = jnp.where(row_no == target, 1.0, 0.0)
    loads[0].wait()
    send1[...] = jnp.dot(
        moved.astype(BF16), cand_v[...], preferred_element_type=F32
    ).astype(BF16)

    pl.semaphore_wait(barrier, caches - 1 + 4)

    def of_user(user):
        return pl.ds(pl.multiple_of(user * cpr, cpr), cpr)

    def of_place(dx, dz, dc):
        return pl.ds(pl.multiple_of(((FAR_X.index(dx) * DEPTHS + dz) * 2 + dc) * cpr, cpr), cpr)

    def send_user(dx, dz, dc):
        peer = peer_at(dx, dz, dc)
        pltpu.make_async_remote_copy(
            src_ref=send1.at[of_user(peer)],
            dst_ref=gathered.at[my_rank, of_place(back(dx, wide), back(dz, DEPTHS), dc)],
            send_sem=a_send,
            recv_sem=a_recv,
            device_id={"cache": peer},
            device_id_type=MESH,
        ).start()

    for_depths(FAR_X, send_user)
    mine, here = of_user(my_cache), of_place(0, 0, 0)
    pltpu.make_async_copy(send1.at[mine], gathered.at[my_rank, here], a_recv).start()

    place[...] = moved.T.astype(BF16)
    for number in (2, 3, 4):
        loads[number].wait()
    length = length_s[0]
    for block in range(hist // BLOCK):
        events = pl.ds(block * BLOCK, BLOCK)
        limit = (length - block * BLOCK) * (mask_s[0, block] == 1).astype(jnp.int32)
        live = (lax.broadcasted_iota(jnp.int32, (BLOCK, head), 0) < limit).astype(F32)
        values_v[events, :] = (values_v[events, :].astype(F32) * live).astype(BF16)
    for number in (5, 6, 7, 8):
        loads[number].wait()
    pltpu.make_async_copy(gathered.at[my_rank], gathered.at[my_rank], a_recv).wait()

    def hop(buffer, phase, chunk, slot, step, recv_sem):
        block = buffer.at[rank_at(slot), pl.ds(chunk * part, part)]
        return pltpu.make_async_remote_copy(
            src_ref=block,
            dst_ref=block,
            send_sem=ring_send.at[phase],
            recv_sem=recv_sem,
            device_id={"rank": rank_at(step)},
            device_id_type=MESH,
        )

    def spread(buffer, phase, chunk):
        for way, step in ((0, 2), (1, -2)):
            hop(buffer, phase, chunk, 0, step, near_recv.at[phase, chunk, way]).start()
        for step in (1, -1):
            hop(buffer, phase, chunk, 0, step, rest_recv.at[phase, chunk]).start()

    def relay(buffer, phase, chunk):
        for way, step in ((0, 1), (1, -1)):
            hop(buffer, phase, chunk, -2 * step, 2 * step, near_recv.at[phase, chunk, way]).wait_recv()
            hop(buffer, phase, chunk, -2 * step, step, rest_recv.at[phase, chunk]).start()
            if chunk % 2 == way:
                hop(buffer, phase, chunk, -2 * step, 2 * step, rest_recv.at[phase, chunk]).start()

    def complete(buffer, phase, chunk):
        five = buffer.at[pl.ds(0, 5), pl.ds(chunk * part, part)]
        pltpu.make_async_copy(five, five, rest_recv.at[phase, chunk]).wait()

    for chunk in range(CHUNKS):
        spread(gathered, 0, chunk)
    for chunk in range(CHUNKS):
        relay(gathered, 0, chunk)

    for chunk in range(CHUNKS):
        complete(gathered, 0, chunk)
        span = pl.ds(chunk * part, part)
        slices = [gathered[k, span, :].astype(F32) for k in range(ranks)]
        centre = jnp.sum(sum(slices[1:], slices[0]), axis=-1, keepdims=True) * (1.0 / (ranks * head))
        slices = [s - centre for s in slices]
        squares = [s * s for s in slices]
        spread_of = jnp.sum(sum(squares[1:], squares[0]), axis=-1, keepdims=True) * (1.0 / (ranks * head))
        factor = lax.rsqrt(spread_of + EPSILON)
        normed = jnp.concatenate([(s * factor).astype(BF16) for s in slices], axis=1)
        both = silu(jnp.dot(normed, w_in_v[...], preferred_element_type=F32))
        queries = both[:, :head].astype(BF16)
        gate = both[:, head:]
        attended = jnp.zeros((part, head), F32)
        for tile in range(hist // KEY_TILE):
            events = pl.ds(tile * KEY_TILE, KEY_TILE)
            scores = lax.dot_general(
                queries, keys_v[events, :], (((1,), (1,)), ((), ())), preferred_element_type=F32
            )
            weights = silu(scores * (head ** -0.5)).astype(BF16)
            attended += jnp.dot(weights, values_v[events, :], preferred_element_type=F32)
        centre = jnp.mean(attended, axis=-1, keepdims=True)
        attended = attended - centre
        spread_of = jnp.mean(attended * attended, axis=-1, keepdims=True)
        hidden[my_rank, span, :] = (attended * lax.rsqrt(spread_of + EPSILON) * gate).astype(BF16)
        spread(hidden, 1, chunk)

    for chunk in range(CHUNKS):
        relay(hidden, 1, chunk)

    for chunk in range(CHUNKS):
        complete(hidden, 1, chunk)
        span = pl.ds(chunk * part, part)
        whole = jnp.concatenate([hidden[k, span, :] for k in range(ranks)], axis=1)
        projected = jnp.dot(whole, w_out_v[...], preferred_element_type=F32)
        send2[span, :] = (gathered[my_rank, span, :].astype(F32) + projected).astype(BF16)

        def send_shard(dx, dz, dc):
            pltpu.make_async_remote_copy(
                src_ref=send2.at[of_place(dx, dz, dc)],
                dst_ref=recv2.at[mine],
                send_sem=b_send,
                recv_sem=b_recv,
                device_id={"cache": peer_at(dx, dz, dc)},
                device_id_type=MESH,
            ).start()

        count = wide // CHUNKS
        for_depths(FAR_X[chunk * count:(chunk + 1) * count], send_shard)
    pltpu.make_async_copy(send2.at[here], recv2.at[mine], b_recv).start()

    pltpu.make_async_copy(recv2, recv2, b_recv).wait()
    ranked[...] = jnp.dot(place[...], recv2[...], preferred_element_type=F32).astype(BF16)

    others = pl.ds(0, rows - cpr)
    pltpu.make_async_copy(send1.at[others], send1.at[others], a_send).wait()
    pltpu.make_async_copy(send2.at[others], send2.at[others], b_send).wait()
    for phase, buffer in ((0, gathered), (1, hidden)):
        seven = buffer.at[pl.ds(0, ranks - 1)]
        pltpu.make_async_copy(seven, seven, ring_send.at[phase]).wait()


def on_device(
    cand_rows, listed, hist_len, block_mask, hist_keys, hist_values, w_query, w_gate, w_out, *, caches, ranks
):
    _, users, cpr, width = cand_rows.shape
    rows = users * cpr
    hist = hist_keys.shape[2]
    depth = w_query.shape[1]
    in_hbm = pl.BlockSpec(memory_space=pltpu.HBM)
    vmem = pl.BlockSpec(memory_space=pltpu.VMEM)
    ranked = pl.pallas_call(
        functools.partial(layer_kernel, caches, ranks, cpr),
        out_shape=jax.ShapeDtypeStruct((rows, width), BF16),
        in_specs=[in_hbm] * 9,
        out_specs=vmem,
        scratch_shapes=[
            pltpu.VMEM((rows, width), BF16),
            pltpu.VMEM((1, users), jnp.int32),
            pltpu.SMEM(hist_len.shape, jnp.int32),
            pltpu.SMEM(block_mask.shape, jnp.int32),
            pltpu.VMEM((hist, width), BF16),
            pltpu.VMEM((hist, width), BF16),
            pltpu.VMEM((depth, 2 * width), BF16),
            pltpu.VMEM((depth, width), BF16),
            pltpu.VMEM((rows, rows), BF16),
            pltpu.VMEM((rows, width), BF16),
            pltpu.VMEM((ranks, rows, width), BF16),
            pltpu.VMEM((ranks, rows, width), BF16),
            pltpu.VMEM((rows, width), BF16),
            pltpu.VMEM((rows, width), BF16),
            pltpu.SemaphoreType.DMA((9,)),
            pltpu.SemaphoreType.DMA,
            pltpu.SemaphoreType.DMA,
            pltpu.SemaphoreType.DMA((2, CHUNKS, 2)),
            pltpu.SemaphoreType.DMA((2, CHUNKS)),
            pltpu.SemaphoreType.DMA((2,)),
            pltpu.SemaphoreType.DMA,
            pltpu.SemaphoreType.DMA,
        ],
        compiler_params=pltpu.CompilerParams(
            collective_id=0, has_side_effects=True, vmem_limit_bytes=(53 * 1024 + 850) * 1024
        ),
        name="hstu_layer",
    )(
        cand_rows.reshape(rows, width),
        listed.reshape(1, users),
        hist_len,
        block_mask,
        hist_keys.reshape(hist, width),
        hist_values.reshape(hist, width),
        w_query.reshape(depth, width),
        w_gate.reshape(depth, width),
        w_out.reshape(depth, width),
    )
    return ranked.reshape(cand_rows.shape)


def solution(mesh):
    placed = (
        P("cache", None, None, "rank"),
        P(),
        P("cache"),
        P("cache", None),
        P(None, "cache", None, "rank"),
        P(None, "cache", None, "rank"),
        P(None, None, "rank"),
        P(None, None, "rank"),
        P(None, None, "rank"),
    )
    return jax.shard_map(
        functools.partial(on_device, caches=mesh.shape["cache"], ranks=mesh.shape["rank"]),
        mesh=mesh,
        in_specs=placed,
        out_specs=P("cache", None, None, "rank"),
        check_vma=False,
    )
```

```python
import functools

import jax
import jax.numpy as jnp
from jax import lax
from jax.experimental import pallas as pl
from jax.experimental.pallas import tpu as pltpu
from jax.sharding import PartitionSpec as P

BLOCK = 128
EPSILON = 1e-05
CHUNKS = 2
PIECES = 4
KEY_TILE = 1024
F32 = jnp.float32
BF16 = jnp.bfloat16


def silu_of_twice(half):
    return half + half * jnp.tanh(half)


DEPTHS = 8
MESH = pl.DeviceIdType.MESH
FAR_X = (2, 1, 3, 0)


def layer_kernel(
    caches, ranks, cpr,
    cand, listed, block_mask, keys, values, w_query, w_gate, w_out, hist_len,
    ranked,
    cand_v, listed_v, mask_s, keys_v, values_v, w_in_v, w_out_v, place, send1, gathered, hidden,
    send2, recv2, load_sem, a_send, a_recv, near_recv, rest_recv, ring_send, b_send, b_recv,
):
    my_cache = lax.axis_index("cache")
    my_rank = lax.axis_index("rank")
    rows = caches * cpr
    part = rows // CHUNKS
    head = keys.shape[1]
    hist = keys.shape[0]
    wide = caches // (2 * DEPTHS)
    my_core = lax.rem(my_cache, 2)
    my_z = lax.rem(my_cache // 2, DEPTHS)
    my_x = my_cache // (2 * DEPTHS)

    barrier = pltpu.get_barrier_semaphore()

    def peer_at(dx, dz, dc):
        x, z, core = lax.rem(my_x + dx, wide), lax.rem(my_z + dz, DEPTHS), lax.rem(my_core + dc, 2)
        return (x * DEPTHS + z) * 2 + core

    def back(step, extent):
        return (extent - step) % extent if isinstance(step, int) else lax.rem(extent - step, extent)

    def for_depths(places, body):
        def one(step, carry):
            away = (step + 1) // 2
            dz = lax.rem(DEPTHS + DEPTHS // 2 + away * (1 - 2 * lax.rem(step, 2)), DEPTHS)
            for dx in places:
                for dc in (0, 1):
                    body(dx, dz, dc)
            return carry

        lax.fori_loop(0, DEPTHS - 1, one, 0)
        for dx in places:
            for dc in (0, 1):
                if (dx, dc) != (0, 0):
                    body(dx, 0, dc)

    def greet(dx, dz, dc):
        pl.semaphore_signal(
            barrier, inc=1, device_id={"cache": peer_at(dx, dz, dc)}, device_id_type=MESH
        )

    for_depths(FAR_X, greet)

    def rank_at(step):
        return lax.rem(my_rank + (step + ranks), ranks)

    for step in (-2, -1, 1, 2):
        pl.semaphore_signal(barrier, inc=1, device_id={"rank": rank_at(step)}, device_id_type=MESH)

    def load(source, target, number):
        return pltpu.make_async_copy(source, target, load_sem.at[number])

    loads = [
        load(cand, cand_v, 0),
        load(listed, listed_v, 1),
        load(values, values_v, 2),
        load(block_mask, mask_s, 3),
        load(keys, keys_v, 4),
        load(w_query, w_in_v.at[:, pl.ds(0, head)], 5),
        load(w_gate, w_in_v.at[:, pl.ds(head, head)], 6),
        load(w_out, w_out_v, 7),
    ]
    for one in loads:
        one.start()

    users = caches
    slot_of = (
        lax.broadcasted_iota(jnp.int32, (users, rows), 1) // cpr
        == lax.broadcasted_iota(jnp.int32, (users, rows), 0)
    ).astype(F32).astype(BF16)
    loads[1].wait()
    listed_rows = jnp.broadcast_to(listed_v[...].astype(F32), (8, users)).astype(BF16)
    user_of = jnp.dot(listed_rows, slot_of, preferred_element_type=F32)[0:1, :]
    column = lax.broadcasted_iota(jnp.int32, (1, rows), 1)
    target = user_of * cpr + lax.rem(column, cpr).astype(F32)
    row_no = lax.broadcasted_iota(jnp.int32, (rows, rows), 0).astype(F32)
    moved = jnp.where(row_no == target, 1.0, 0.0)
    loads[0].wait()
    send1[...] = jnp.dot(
        moved.astype(BF16), cand_v[...], preferred_element_type=F32
    ).astype(BF16)

    pl.semaphore_wait(barrier, caches - 1 + 4)

    def of_user(user):
        return pl.ds(pl.multiple_of(user * cpr, cpr), cpr)

    def of_place(dx, dz, dc):
        return pl.ds(pl.multiple_of(((FAR_X.index(dx) * DEPTHS + dz) * 2 + dc) * cpr, cpr), cpr)

    def send_user(dx, dz, dc):
        peer = peer_at(dx, dz, dc)
        pltpu.make_async_remote_copy(
            src_ref=send1.at[of_user(peer)],
            dst_ref=gathered.at[my_rank, of_place(back(dx, wide), back(dz, DEPTHS), dc)],
            send_sem=a_send,
            recv_sem=a_recv,
            device_id={"cache": peer},
            device_id_type=MESH,
        ).start()

    for_depths(FAR_X, send_user)
    mine, here = of_user(my_cache), of_place(0, 0, 0)
    pltpu.make_async_copy(send1.at[mine], gathered.at[my_rank, here], a_recv).start()

    place[...] = moved.T.astype(BF16)
    for number in (2, 3):
        loads[number].wait()
    length = hist_len[0]
    for block in range(hist // BLOCK):
        events = pl.ds(block * BLOCK, BLOCK)
        limit = (length - block * BLOCK) * (mask_s[0, block] == 1).astype(jnp.int32)
        live = (lax.broadcasted_iota(jnp.int32, (BLOCK, head), 0) < limit).astype(F32)
        values_v[events, :] = (values_v[events, :].astype(F32) * live).astype(BF16)
    for number in (4, 5, 6, 7):
        loads[number].wait()
    pltpu.make_async_copy(gathered.at[my_rank], gathered.at[my_rank], a_recv).wait()

    small = rows // PIECES
    of_chunk = [range(c * PIECES // CHUNKS, (c + 1) * PIECES // CHUNKS) for c in range(CHUNKS)]

    def hop(buffer, phase, piece, slot, step, recv_sem):
        block = buffer.at[rank_at(slot), pl.ds(piece * small, small)]
        return pltpu.make_async_remote_copy(
            src_ref=block,
            dst_ref=block,
            send_sem=ring_send.at[phase],
            recv_sem=recv_sem,
            device_id={"rank": rank_at(step)},
            device_id_type=MESH,
        )

    def spread_near(buffer, phase, chunk):
        for piece in of_chunk[chunk]:
            for way, step in ((0, 2), (1, -2)):
                hop(buffer, phase, piece, 0, step, near_recv.at[phase, piece, way]).start()

    def spread_next(buffer, phase, chunk):
        for piece in of_chunk[chunk]:
            for step in (1, -1):
                hop(buffer, phase, piece, 0, step, rest_recv.at[phase, chunk]).start()

    def relay(buffer, phase, chunk):
        for piece in of_chunk[chunk]:
            for way, step in ((0, 1), (1, -1)):
                hop(buffer, phase, piece, -2 * step, 2 * step, near_recv.at[phase, piece, way]).wait_recv()
                hop(buffer, phase, piece, -2 * step, step, rest_recv.at[phase, chunk]).start()
                if piece % 2 == way:
                    hop(buffer, phase, piece, -2 * step, 2 * step, rest_recv.at[phase, chunk]).start()

    def complete(buffer, phase, chunk):
        five = buffer.at[pl.ds(0, 5), pl.ds(chunk * part, part)]
        pltpu.make_async_copy(five, five, rest_recv.at[phase, chunk]).wait()

    for chunk in range(CHUNKS):
        spread_near(gathered, 0, chunk)
    for chunk in range(CHUNKS):
        spread_next(gathered, 0, chunk)
    for chunk in range(CHUNKS):
        relay(gathered, 0, chunk)

    for chunk in range(CHUNKS):
        complete(gathered, 0, chunk)
        span = pl.ds(chunk * part, part)
        slices = [gathered[k, span, :].astype(F32) for k in range(ranks)]
        centre = jnp.sum(sum(slices[1:], slices[0]), axis=-1, keepdims=True) * (1.0 / (ranks * head))
        slices = [s - centre for s in slices]
        squares = [s * s for s in slices]
        spread_of = jnp.sum(sum(squares[1:], squares[0]), axis=-1, keepdims=True) * (1.0 / (ranks * head))
        factor = lax.rsqrt(spread_of + EPSILON)
        normed = jnp.concatenate([(s * factor).astype(BF16) for s in slices], axis=1)
        both = silu_of_twice(0.5 * jnp.dot(normed, w_in_v[...], preferred_element_type=F32))
        queries = both[:, :head].astype(BF16)
        gate = both[:, head:]
        attended = jnp.zeros((part, head), F32)
        for tile in range(hist // KEY_TILE):
            events = pl.ds(tile * KEY_TILE, KEY_TILE)
            scores = lax.dot_general(
                queries, keys_v[events, :], (((1,), (1,)), ((), ())), preferred_element_type=F32
            )
            weights = silu_of_twice(scores * (0.5 * head ** -0.5)).astype(BF16)
            attended += jnp.dot(weights, values_v[events, :], preferred_element_type=F32)
        centre = jnp.mean(attended, axis=-1, keepdims=True)
        attended = attended - centre
        spread_of = jnp.mean(attended * attended, axis=-1, keepdims=True)
        hidden[my_rank, span, :] = (attended * lax.rsqrt(spread_of + EPSILON) * gate).astype(BF16)
        spread_near(hidden, 1, chunk)
        spread_next(hidden, 1, chunk)

    for chunk in range(CHUNKS):
        relay(hidden, 1, chunk)

    for chunk in range(CHUNKS):
        complete(hidden, 1, chunk)
        span = pl.ds(chunk * part, part)
        whole = jnp.concatenate([hidden[k, span, :] for k in range(ranks)], axis=1)
        projected = jnp.dot(whole, w_out_v[...], preferred_element_type=F32)
        send2[span, :] = (gathered[my_rank, span, :].astype(F32) + projected).astype(BF16)

        def send_shard(dx, dz, dc):
            pltpu.make_async_remote_copy(
                src_ref=send2.at[of_place(dx, dz, dc)],
                dst_ref=recv2.at[mine],
                send_sem=b_send,
                recv_sem=b_recv,
                device_id={"cache": peer_at(dx, dz, dc)},
                device_id_type=MESH,
            ).start()

        count = wide // CHUNKS
        for_depths(FAR_X[chunk * count:(chunk + 1) * count], send_shard)
    pltpu.make_async_copy(send2.at[here], recv2.at[mine], b_recv).start()

    pltpu.make_async_copy(recv2, recv2, b_recv).wait()
    ranked[...] = jnp.dot(place[...], recv2[...], preferred_element_type=F32).astype(BF16)

    others = pl.ds(0, rows - cpr)
    pltpu.make_async_copy(send1.at[others], send1.at[others], a_send).wait()
    pltpu.make_async_copy(send2.at[others], send2.at[others], b_send).wait()
    for phase, buffer in ((0, gathered), (1, hidden)):
        seven = buffer.at[pl.ds(0, ranks - 1)]
        pltpu.make_async_copy(seven, seven, ring_send.at[phase]).wait()


def on_device(
    cand_rows, listed, hist_len, block_mask, hist_keys, hist_values, w_query, w_gate, w_out, *, caches, ranks
):
    _, users, cpr, width = cand_rows.shape
    rows = users * cpr
    hist = hist_keys.shape[2]
    depth = w_query.shape[1]
    in_hbm = pl.BlockSpec(memory_space=pltpu.HBM)
    vmem = pl.BlockSpec(memory_space=pltpu.VMEM)
    ranked = pl.pallas_call(
        functools.partial(layer_kernel, caches, ranks, cpr),
        out_shape=jax.ShapeDtypeStruct((rows, width), BF16),
        in_specs=[in_hbm] * 8 + [pl.BlockSpec(memory_space=pltpu.SMEM)],
        out_specs=vmem,
        scratch_shapes=[
            pltpu.VMEM((rows, width), BF16),
            pltpu.VMEM((1, users), jnp.int32),
            pltpu.SMEM(block_mask.shape, jnp.int32),
            pltpu.VMEM((hist, width), BF16),
            pltpu.VMEM((hist, width), BF16),
            pltpu.VMEM((depth, 2 * width), BF16),
            pltpu.VMEM((depth, width), BF16),
            pltpu.VMEM((rows, rows), BF16),
            pltpu.VMEM((rows, width), BF16),
            pltpu.VMEM((ranks, rows, width), BF16),
            pltpu.VMEM((ranks, rows, width), BF16),
            pltpu.VMEM((rows, width), BF16),
            pltpu.VMEM((rows, width), BF16),
            pltpu.SemaphoreType.DMA((8,)),
            pltpu.SemaphoreType.DMA,
            pltpu.SemaphoreType.DMA,
            pltpu.SemaphoreType.DMA((2, PIECES, 2)),
            pltpu.SemaphoreType.DMA((2, CHUNKS)),
            pltpu.SemaphoreType.DMA((2,)),
            pltpu.SemaphoreType.DMA,
            pltpu.SemaphoreType.DMA,
        ],
        compiler_params=pltpu.CompilerParams(
            collective_id=0, has_side_effects=True, vmem_limit_bytes=40 * 1024 * 1024
        ),
        name="hstu_layer",
    )(
        *(
            pltpu.with_memory_space_constraint(array, pltpu.HBM)
            for array in (
                cand_rows.reshape(rows, width),
                listed.reshape(1, users),
                block_mask,
                hist_keys.reshape(hist, width),
                hist_values.reshape(hist, width),
                w_query.reshape(depth, width),
                w_gate.reshape(depth, width),
                w_out.reshape(depth, width),
            )
        ),
        hist_len,
    )
    return ranked.reshape(cand_rows.shape)


def solution(mesh):
    placed = (
        P("cache", None, None, "rank"),
        P(),
        P("cache"),
        P("cache", None),
        P(None, "cache", None, "rank"),
        P(None, "cache", None, "rank"),
        P(None, None, "rank"),
        P(None, None, "rank"),
        P(None, None, "rank"),
    )
    return jax.shard_map(
        functools.partial(on_device, caches=mesh.shape["cache"], ranks=mesh.shape["rank"]),
        mesh=mesh,
        in_specs=placed,
        out_specs=P("cache", None, None, "rank"),
        check_vma=False,
    )
```

```python
import functools

import jax
import jax.numpy as jnp
from jax import lax
from jax.experimental import pallas as pl
from jax.experimental.pallas import tpu as pltpu
from jax.sharding import PartitionSpec as P

BLOCK = 128
EPSILON = 1e-05
PIECES = 4
GROUPS = ((0, 1), (2, 3))
CHUNKS = ((0,), (1,))
KEY_TILE = 1024
F32 = jnp.float32
BF16 = jnp.bfloat16


def silu_of_twice(half):
    return half + half * jnp.tanh(half)


DEPTHS = 8
MESH = pl.DeviceIdType.MESH
FAR_X = (2, 1, 3, 0)


def layer_kernel(
    caches, ranks, cpr,
    cand, listed, block_mask, keys, values, w_query, w_gate, w_out, hist_len,
    ranked,
    cand_v, listed_v, mask_s, keys_v, values_v, w_in_v, w_out_v, place, send1, gathered, hidden,
    send2, recv2, load_sem, a_send, a_recv, near_recv, rest_recv, ring_send, b_send, b_recv,
):
    my_cache = lax.axis_index("cache")
    my_rank = lax.axis_index("rank")
    rows = caches * cpr
    head = keys.shape[1]
    hist = keys.shape[0]
    wide = caches // (2 * DEPTHS)
    my_core = lax.rem(my_cache, 2)
    my_z = lax.rem(my_cache // 2, DEPTHS)
    my_x = my_cache // (2 * DEPTHS)

    barrier = pltpu.get_barrier_semaphore()

    def peer_at(dx, dz, dc):
        x, z, core = lax.rem(my_x + dx, wide), lax.rem(my_z + dz, DEPTHS), lax.rem(my_core + dc, 2)
        return (x * DEPTHS + z) * 2 + core

    def back(step, extent):
        return (extent - step) % extent if isinstance(step, int) else lax.rem(extent - step, extent)

    def for_depths(places, body):
        def one(step, carry):
            away = (step + 1) // 2
            dz = lax.rem(DEPTHS + DEPTHS // 2 + away * (1 - 2 * lax.rem(step, 2)), DEPTHS)
            for dx in places:
                for dc in (0, 1):
                    body(dx, dz, dc)
            return carry

        lax.fori_loop(0, DEPTHS - 1, one, 0)
        for dx in places:
            for dc in (0, 1):
                if (dx, dc) != (0, 0):
                    body(dx, 0, dc)

    def greet(dx, dz, dc):
        pl.semaphore_signal(
            barrier, inc=1, device_id={"cache": peer_at(dx, dz, dc)}, device_id_type=MESH
        )

    for_depths(FAR_X, greet)

    def rank_at(step):
        return lax.rem(my_rank + (step + ranks), ranks)

    for step in (-2, -1, 1, 2):
        pl.semaphore_signal(barrier, inc=1, device_id={"rank": rank_at(step)}, device_id_type=MESH)

    def load(source, target, number):
        return pltpu.make_async_copy(source, target, load_sem.at[number])

    loads = [
        load(cand, cand_v, 0),
        load(listed, listed_v, 1),
        load(values, values_v, 2),
        load(block_mask, mask_s, 3),
        load(keys, keys_v, 4),
        load(w_query, w_in_v.at[:, pl.ds(0, head)], 5),
        load(w_gate, w_in_v.at[:, pl.ds(head, head)], 6),
        load(w_out, w_out_v, 7),
    ]
    for one in loads:
        one.start()

    users = caches
    slot_of = (
        lax.broadcasted_iota(jnp.int32, (users, rows), 1) // cpr
        == lax.broadcasted_iota(jnp.int32, (users, rows), 0)
    ).astype(F32).astype(BF16)
    loads[1].wait()
    listed_rows = jnp.broadcast_to(listed_v[...].astype(F32), (8, users)).astype(BF16)
    user_of = jnp.dot(listed_rows, slot_of, preferred_element_type=F32)[0:1, :]
    column = lax.broadcasted_iota(jnp.int32, (1, rows), 1)
    target = user_of * cpr + lax.rem(column, cpr).astype(F32)
    row_no = lax.broadcasted_iota(jnp.int32, (rows, rows), 0).astype(F32)
    moved = jnp.where(row_no == target, 1.0, 0.0)
    loads[0].wait()
    send1[...] = jnp.dot(
        moved.astype(BF16), cand_v[...], preferred_element_type=F32
    ).astype(BF16)

    pl.semaphore_wait(barrier, caches - 1 + 4)

    def of_user(user):
        return pl.ds(pl.multiple_of(user * cpr, cpr), cpr)

    def of_place(dx, dz, dc):
        return pl.ds(pl.multiple_of(((FAR_X.index(dx) * DEPTHS + dz) * 2 + dc) * cpr, cpr), cpr)

    def send_user(dx, dz, dc):
        peer = peer_at(dx, dz, dc)
        pltpu.make_async_remote_copy(
            src_ref=send1.at[of_user(peer)],
            dst_ref=gathered.at[my_rank, of_place(back(dx, wide), back(dz, DEPTHS), dc)],
            send_sem=a_send,
            recv_sem=a_recv,
            device_id={"cache": peer},
            device_id_type=MESH,
        ).start()

    for_depths(FAR_X, send_user)
    mine, here = of_user(my_cache), of_place(0, 0, 0)
    pltpu.make_async_copy(send1.at[mine], gathered.at[my_rank, here], a_recv).start()

    place[...] = moved.T.astype(BF16)
    for number in (2, 3):
        loads[number].wait()
    length = hist_len[0]
    for block in range(hist // BLOCK):
        events = pl.ds(block * BLOCK, BLOCK)
        limit = (length - block * BLOCK) * (mask_s[0, block] == 1).astype(jnp.int32)
        live = (lax.broadcasted_iota(jnp.int32, (BLOCK, head), 0) < limit).astype(F32)
        values_v[events, :] = (values_v[events, :].astype(F32) * live).astype(BF16)
    for number in (4, 5, 6, 7):
        loads[number].wait()
    pltpu.make_async_copy(gathered.at[my_rank], gathered.at[my_rank], a_recv).wait()

    small = rows // PIECES

    group_of = {piece: number for number, group in enumerate(GROUPS) for piece in group}

    def span_of(pieces):
        return pl.ds(pieces[0] * small, len(pieces) * small)

    def hop(buffer, phase, piece, slot, step, recv_sem):
        block = buffer.at[rank_at(slot), pl.ds(piece * small, small)]
        return pltpu.make_async_remote_copy(
            src_ref=block,
            dst_ref=block,
            send_sem=ring_send.at[phase],
            recv_sem=recv_sem,
            device_id={"rank": rank_at(step)},
            device_id_type=MESH,
        )

    def rest(phase, piece):
        return rest_recv.at[phase, group_of[piece]]

    def spread_near(buffer, phase, pieces):
        for piece in pieces:
            for way, step in ((0, 2), (1, -2)):
                hop(buffer, phase, piece, 0, step, near_recv.at[phase, piece, way]).start()

    def spread_next(buffer, phase, pieces):
        for piece in pieces:
            for step in (1, -1):
                hop(buffer, phase, piece, 0, step, rest(phase, piece)).start()

    def relay(buffer, phase, pieces):
        for piece in pieces:
            for way, step in ((0, 1), (1, -1)):
                hop(buffer, phase, piece, -2 * step, 2 * step, near_recv.at[phase, piece, way]).wait_recv()
                if piece % 2 == way:
                    hop(buffer, phase, piece, -2 * step, 2 * step, rest(phase, piece)).start()
                hop(buffer, phase, piece, -2 * step, step, rest(phase, piece)).start()

    def complete(buffer, phase, group):
        five = buffer.at[pl.ds(0, 5), span_of(GROUPS[group])]
        pltpu.make_async_copy(five, five, rest_recv.at[phase, group]).wait()

    def exchange(buffer, phase):
        every = range(PIECES)
        spread_next(buffer, phase, every[:-1])
        relay(buffer, phase, every)
        spread_next(buffer, phase, every[-1:])

    def pieces_of(chunk):
        return [piece for group in chunk for piece in GROUPS[group]]

    spread_near(gathered, 0, range(PIECES))
    exchange(gathered, 0)

    for chunk in CHUNKS:
        for group in chunk:
            complete(gathered, 0, group)
        span = span_of(pieces_of(chunk))
        slices = [gathered[k, span, :].astype(F32) for k in range(ranks)]
        centre = jnp.sum(sum(slices[1:], slices[0]), axis=-1, keepdims=True) * (1.0 / (ranks * head))
        slices = [s - centre for s in slices]
        squares = [s * s for s in slices]
        spread_of = jnp.sum(sum(squares[1:], squares[0]), axis=-1, keepdims=True) * (1.0 / (ranks * head))
        factor = lax.rsqrt(spread_of + EPSILON)
        normed = jnp.concatenate([(s * factor).astype(BF16) for s in slices], axis=1)
        both = silu_of_twice(0.5 * jnp.dot(normed, w_in_v[...], preferred_element_type=F32))
        queries = both[:, :head].astype(BF16)
        gate = both[:, head:]
        attended = jnp.zeros((span.size, head), F32)
        for tile in range(hist // KEY_TILE):
            events = pl.ds(tile * KEY_TILE, KEY_TILE)
            scores = lax.dot_general(
                queries, keys_v[events, :], (((1,), (1,)), ((), ())), preferred_element_type=F32
            )
            weights = silu_of_twice(scores * (0.5 * head ** -0.5)).astype(BF16)
            attended += jnp.dot(weights, values_v[events, :], preferred_element_type=F32)
        centre = jnp.mean(attended, axis=-1, keepdims=True)
        attended = attended - centre
        spread_of = jnp.mean(attended * attended, axis=-1, keepdims=True)
        hidden[my_rank, span, :] = (attended * lax.rsqrt(spread_of + EPSILON) * gate).astype(BF16)
        spread_near(hidden, 1, pieces_of(chunk))

    exchange(hidden, 1)

    for group, pieces in enumerate(GROUPS):
        complete(hidden, 1, group)
        span = span_of(pieces)
        whole = jnp.concatenate([hidden[k, span, :] for k in range(ranks)], axis=1)
        projected = jnp.dot(whole, w_out_v[...], preferred_element_type=F32)
        send2[span, :] = (gathered[my_rank, span, :].astype(F32) + projected).astype(BF16)

        def send_shard(dx, dz, dc):
            pltpu.make_async_remote_copy(
                src_ref=send2.at[of_place(dx, dz, dc)],
                dst_ref=recv2.at[mine],
                send_sem=b_send,
                recv_sem=b_recv,
                device_id={"cache": peer_at(dx, dz, dc)},
                device_id_type=MESH,
            ).start()

        for_depths([FAR_X[piece] for piece in pieces], send_shard)
    pltpu.make_async_copy(send2.at[here], recv2.at[mine], b_recv).start()

    pltpu.make_async_copy(recv2, recv2, b_recv).wait()
    ranked[...] = jnp.dot(place[...], recv2[...], preferred_element_type=F32).astype(BF16)

    others = pl.ds(0, rows - cpr)
    pltpu.make_async_copy(send1.at[others], send1.at[others], a_send).wait()
    pltpu.make_async_copy(send2.at[others], send2.at[others], b_send).wait()
    for phase, buffer in ((0, gathered), (1, hidden)):
        seven = buffer.at[pl.ds(0, ranks - 1)]
        pltpu.make_async_copy(seven, seven, ring_send.at[phase]).wait()


def on_device(
    cand_rows, listed, hist_len, block_mask, hist_keys, hist_values, w_query, w_gate, w_out, *, caches, ranks
):
    _, users, cpr, width = cand_rows.shape
    rows = users * cpr
    hist = hist_keys.shape[2]
    depth = w_query.shape[1]
    in_hbm = pl.BlockSpec(memory_space=pltpu.HBM)
    vmem = pl.BlockSpec(memory_space=pltpu.VMEM)
    ranked = pl.pallas_call(
        functools.partial(layer_kernel, caches, ranks, cpr),
        out_shape=jax.ShapeDtypeStruct((rows, width), BF16),
        in_specs=[in_hbm] * 8 + [pl.BlockSpec(memory_space=pltpu.SMEM)],
        out_specs=vmem,
        scratch_shapes=[
            pltpu.VMEM((rows, width), BF16),
            pltpu.VMEM((1, users), jnp.int32),
            pltpu.SMEM(block_mask.shape, jnp.int32),
            pltpu.VMEM((hist, width), BF16),
            pltpu.VMEM((hist, width), BF16),
            pltpu.VMEM((depth, 2 * width), BF16),
            pltpu.VMEM((depth, width), BF16),
            pltpu.VMEM((rows, rows), BF16),
            pltpu.VMEM((rows, width), BF16),
            pltpu.VMEM((ranks, rows, width), BF16),
            pltpu.VMEM((ranks, rows, width), BF16),
            pltpu.VMEM((rows, width), BF16),
            pltpu.VMEM((rows, width), BF16),
            pltpu.SemaphoreType.DMA((8,)),
            pltpu.SemaphoreType.DMA,
            pltpu.SemaphoreType.DMA,
            pltpu.SemaphoreType.DMA((2, PIECES, 2)),
            pltpu.SemaphoreType.DMA((2, len(GROUPS))),
            pltpu.SemaphoreType.DMA((2,)),
            pltpu.SemaphoreType.DMA,
            pltpu.SemaphoreType.DMA,
        ],
        compiler_params=pltpu.CompilerParams(
            collective_id=0, has_side_effects=True, vmem_limit_bytes=40 * 1024 * 1024
        ),
        name="hstu_layer",
    )(
        *(
            pltpu.with_memory_space_constraint(array, pltpu.HBM)
            for array in (
                cand_rows.reshape(rows, width),
                listed.reshape(1, users),
                block_mask,
                hist_keys.reshape(hist, width),
                hist_values.reshape(hist, width),
                w_query.reshape(depth, width),
                w_gate.reshape(depth, width),
                w_out.reshape(depth, width),
            )
        ),
        hist_len,
    )
    return ranked.reshape(cand_rows.shape)


def solution(mesh):
    placed = (
        P("cache", None, None, "rank"),
        P(),
        P("cache"),
        P("cache", None),
        P(None, "cache", None, "rank"),
        P(None, "cache", None, "rank"),
        P(None, None, "rank"),
        P(None, None, "rank"),
        P(None, None, "rank"),
    )
    return jax.shard_map(
        functools.partial(on_device, caches=mesh.shape["cache"], ranks=mesh.shape["rank"]),
        mesh=mesh,
        in_specs=placed,
        out_specs=P("cache", None, None, "rank"),
        check_vma=False,
    )
```

```python
import functools

import jax
import jax.numpy as jnp
from jax import lax
from jax.experimental import pallas as pl
from jax.experimental.pallas import tpu as pltpu
from jax.sharding import PartitionSpec as P

BLOCK = 128
EPSILON = 1e-05
PIECES = 4
GROUPS = ((0, 1), (2, 3))
CHUNKS = ((0,), (1,))
KEY_TILE = 1024
F32 = jnp.float32
BF16 = jnp.bfloat16


def silu_of_twice(half):
    return half + half * jnp.tanh(half)


DEPTHS = 8
MESH = pl.DeviceIdType.MESH
FAR_X = (2, 1, 3, 0)


def layer_kernel(
    caches, ranks, cpr,
    cand, listed, block_mask, keys, values, w_query, w_gate, w_out, hist_len,
    ranked,
    cand_v, listed_v, mask_s, keys_v, values_v, w_in_v, w_out_v, place, send1, gathered, hidden,
    send2, recv2, load_sem, a_send, a_recv, near_recv, rest_recv, ring_send, b_send, b_recv,
):
    my_cache = lax.axis_index("cache")
    my_rank = lax.axis_index("rank")
    rows = caches * cpr
    head = keys.shape[1]
    hist = keys.shape[0]
    wide = caches // (2 * DEPTHS)
    my_core = lax.rem(my_cache, 2)
    my_z = lax.rem(my_cache // 2, DEPTHS)
    my_x = my_cache // (2 * DEPTHS)

    barrier = pltpu.get_barrier_semaphore()

    def peer_at(dx, dz, dc):
        x, z, core = lax.rem(my_x + dx, wide), lax.rem(my_z + dz, DEPTHS), lax.rem(my_core + dc, 2)
        return (x * DEPTHS + z) * 2 + core

    def back(step, extent):
        return (extent - step) % extent if isinstance(step, int) else lax.rem(extent - step, extent)

    def for_depths(places, body):
        def one(step, carry):
            away = (step + 1) // 2
            dz = lax.rem(DEPTHS + DEPTHS // 2 + away * (1 - 2 * lax.rem(step, 2)), DEPTHS)
            for dx in places:
                for dc in (0, 1):
                    body(dx, dz, dc)
            return carry

        lax.fori_loop(0, DEPTHS - 1, one, 0)
        for dx in places:
            for dc in (0, 1):
                if (dx, dc) != (0, 0):
                    body(dx, 0, dc)

    def greet(dx, dz, dc):
        pl.semaphore_signal(
            barrier, inc=1, device_id={"cache": peer_at(dx, dz, dc)}, device_id_type=MESH
        )

    def rank_at(step):
        return lax.rem(my_rank + (step + ranks), ranks)

    def load(source, target, number):
        return pltpu.make_async_copy(source, target, load_sem.at[number])

    loads = [
        load(cand, cand_v, 0),
        load(listed, listed_v, 1),
        load(values, values_v, 2),
        load(block_mask, mask_s, 3),
        load(keys, keys_v, 4),
        load(w_query, w_in_v.at[:, pl.ds(0, head)], 5),
        load(w_gate, w_in_v.at[:, pl.ds(head, head)], 6),
        load(w_out, w_out_v, 7),
    ]

    for one in loads[:2]:
        one.start()
    for_depths(FAR_X, greet)
    for step in (-2, -1, 1, 2):
        pl.semaphore_signal(barrier, inc=1, device_id={"rank": rank_at(step)}, device_id_type=MESH)
    for one in loads[2:]:
        one.start()

    users = caches
    slot_of = (
        lax.broadcasted_iota(jnp.int32, (users, rows), 1) // cpr
        == lax.broadcasted_iota(jnp.int32, (users, rows), 0)
    ).astype(F32).astype(BF16)
    loads[1].wait()
    listed_rows = jnp.broadcast_to(listed_v[...].astype(F32), (8, users)).astype(BF16)
    user_of = jnp.dot(listed_rows, slot_of, preferred_element_type=F32)[0:1, :]
    column = lax.broadcasted_iota(jnp.int32, (1, rows), 1)
    target = user_of * cpr + lax.rem(column, cpr).astype(F32)
    row_no = lax.broadcasted_iota(jnp.int32, (rows, rows), 0).astype(F32)
    moved = jnp.where(row_no == target, 1.0, 0.0)
    loads[0].wait()
    send1[...] = jnp.dot(
        moved.astype(BF16), cand_v[...], preferred_element_type=F32
    ).astype(BF16)

    pl.semaphore_wait(barrier, caches - 1 + 4)

    def of_user(user):
        return pl.ds(pl.multiple_of(user * cpr, cpr), cpr)

    def of_place(dx, dz, dc):
        return pl.ds(pl.multiple_of(((FAR_X.index(dx) * DEPTHS + dz) * 2 + dc) * cpr, cpr), cpr)

    def send_user(dx, dz, dc):
        peer = peer_at(dx, dz, dc)
        pltpu.make_async_remote_copy(
            src_ref=send1.at[of_user(peer)],
            dst_ref=gathered.at[my_rank, of_place(back(dx, wide), back(dz, DEPTHS), dc)],
            send_sem=a_send,
            recv_sem=a_recv,
            device_id={"cache": peer},
            device_id_type=MESH,
        ).start()

    for_depths(FAR_X, send_user)
    mine, here = of_user(my_cache), of_place(0, 0, 0)
    pltpu.make_async_copy(send1.at[mine], gathered.at[my_rank, here], a_recv).start()

    place[...] = moved.T.astype(BF16)
    for number in (2, 3):
        loads[number].wait()
    length = hist_len[0]
    for block in range(hist // BLOCK):
        events = pl.ds(block * BLOCK, BLOCK)
        limit = (length - block * BLOCK) * (mask_s[0, block] == 1).astype(jnp.int32)
        live = (lax.broadcasted_iota(jnp.int32, (BLOCK, head), 0) < limit).astype(F32)
        values_v[events, :] = (values_v[events, :].astype(F32) * live).astype(BF16)
    for number in (4, 5, 6, 7):
        loads[number].wait()
    pltpu.make_async_copy(gathered.at[my_rank], gathered.at[my_rank], a_recv).wait()

    small = rows // PIECES

    group_of = {piece: number for number, group in enumerate(GROUPS) for piece in group}

    def span_of(pieces):
        return pl.ds(pieces[0] * small, len(pieces) * small)

    def hop(buffer, phase, piece, slot, step, recv_sem):
        block = buffer.at[rank_at(slot), pl.ds(piece * small, small)]
        return pltpu.make_async_remote_copy(
            src_ref=block,
            dst_ref=block,
            send_sem=ring_send.at[phase],
            recv_sem=recv_sem,
            device_id={"rank": rank_at(step)},
            device_id_type=MESH,
        )

    def rest(phase, piece):
        return rest_recv.at[phase, group_of[piece]]

    def spread_near(buffer, phase, pieces):
        for piece in pieces:
            for way, step in ((0, 2), (1, -2)):
                hop(buffer, phase, piece, 0, step, near_recv.at[phase, piece, way]).start()

    def spread_next(buffer, phase, pieces):
        for piece in pieces:
            for step in (1, -1):
                hop(buffer, phase, piece, 0, step, rest(phase, piece)).start()

    def relay(buffer, phase, pieces):
        for piece in pieces:
            for way, step in ((0, 1), (1, -1)):
                hop(buffer, phase, piece, -2 * step, 2 * step, near_recv.at[phase, piece, way]).wait_recv()
                if piece % 2 == way:
                    hop(buffer, phase, piece, -2 * step, 2 * step, rest(phase, piece)).start()
                hop(buffer, phase, piece, -2 * step, step, rest(phase, piece)).start()

    def complete(buffer, phase, group):
        five = buffer.at[pl.ds(0, 5), span_of(GROUPS[group])]
        pltpu.make_async_copy(five, five, rest_recv.at[phase, group]).wait()

    def exchange(buffer, phase):
        every = range(PIECES)
        spread_next(buffer, phase, every[:-1])
        relay(buffer, phase, every)
        spread_next(buffer, phase, every[-1:])

    def pieces_of(chunk):
        return [piece for group in chunk for piece in GROUPS[group]]

    spread_near(gathered, 0, range(PIECES))
    exchange(gathered, 0)

    for chunk in CHUNKS:
        for group in chunk:
            complete(gathered, 0, group)
        span = span_of(pieces_of(chunk))
        slices = [gathered[k, span, :].astype(F32) for k in range(ranks)]
        centre = jnp.sum(sum(slices[1:], slices[0]), axis=-1, keepdims=True) * (1.0 / (ranks * head))
        slices = [s - centre for s in slices]
        squares = [s * s for s in slices]
        spread_of = jnp.sum(sum(squares[1:], squares[0]), axis=-1, keepdims=True) * (1.0 / (ranks * head))
        factor = lax.rsqrt(spread_of + EPSILON)
        normed = jnp.concatenate([(s * factor).astype(BF16) for s in slices], axis=1)
        both = silu_of_twice(0.5 * jnp.dot(normed, w_in_v[...], preferred_element_type=F32))
        queries = both[:, :head].astype(BF16)
        gate = both[:, head:]
        attended = jnp.zeros((span.size, head), F32)
        for tile in range(hist // KEY_TILE):
            events = pl.ds(tile * KEY_TILE, KEY_TILE)
            scores = lax.dot_general(
                queries, keys_v[events, :], (((1,), (1,)), ((), ())), preferred_element_type=F32
            )
            weights = silu_of_twice(scores * (0.5 * head ** -0.5)).astype(BF16)
            attended += jnp.dot(weights, values_v[events, :], preferred_element_type=F32)
        centre = jnp.mean(attended, axis=-1, keepdims=True)
        attended = attended - centre
        spread_of = jnp.mean(attended * attended, axis=-1, keepdims=True)
        hidden[my_rank, span, :] = (attended * lax.rsqrt(spread_of + EPSILON) * gate).astype(BF16)
        spread_near(hidden, 1, pieces_of(chunk))

    exchange(hidden, 1)

    for group, pieces in enumerate(GROUPS):
        complete(hidden, 1, group)
        span = span_of(pieces)
        whole = jnp.concatenate([hidden[k, span, :] for k in range(ranks)], axis=1)
        projected = jnp.dot(whole, w_out_v[...], preferred_element_type=F32)
        send2[span, :] = (gathered[my_rank, span, :].astype(F32) + projected).astype(BF16)

        def send_shard(dx, dz, dc):
            pltpu.make_async_remote_copy(
                src_ref=send2.at[of_place(dx, dz, dc)],
                dst_ref=recv2.at[mine],
                send_sem=b_send,
                recv_sem=b_recv,
                device_id={"cache": peer_at(dx, dz, dc)},
                device_id_type=MESH,
            ).start()

        for_depths([FAR_X[piece] for piece in pieces], send_shard)
    pltpu.make_async_copy(send2.at[here], recv2.at[mine], b_recv).start()

    pltpu.make_async_copy(recv2, recv2, b_recv).wait()
    ranked[...] = jnp.dot(place[...], recv2[...], preferred_element_type=F32).astype(BF16)

    others = pl.ds(0, rows - cpr)
    pltpu.make_async_copy(send1.at[others], send1.at[others], a_send).wait()
    pltpu.make_async_copy(send2.at[others], send2.at[others], b_send).wait()
    for phase, buffer in ((0, gathered), (1, hidden)):
        seven = buffer.at[pl.ds(0, ranks - 1)]
        pltpu.make_async_copy(seven, seven, ring_send.at[phase]).wait()


def on_device(
    cand_rows, listed, hist_len, block_mask, hist_keys, hist_values, w_query, w_gate, w_out, *, caches, ranks
):
    _, users, cpr, width = cand_rows.shape
    rows = users * cpr
    hist = hist_keys.shape[2]
    depth = w_query.shape[1]
    in_hbm = pl.BlockSpec(memory_space=pltpu.HBM)
    vmem = pl.BlockSpec(memory_space=pltpu.VMEM)
    ranked = pl.pallas_call(
        functools.partial(layer_kernel, caches, ranks, cpr),
        out_shape=jax.ShapeDtypeStruct((rows, width), BF16),
        in_specs=[in_hbm] * 8 + [pl.BlockSpec(memory_space=pltpu.SMEM)],
        out_specs=vmem,
        scratch_shapes=[
            pltpu.VMEM((rows, width), BF16),
            pltpu.VMEM((1, users), jnp.int32),
            pltpu.SMEM(block_mask.shape, jnp.int32),
            pltpu.VMEM((hist, width), BF16),
            pltpu.VMEM((hist, width), BF16),
            pltpu.VMEM((depth, 2 * width), BF16),
            pltpu.VMEM((depth, width), BF16),
            pltpu.VMEM((rows, rows), BF16),
            pltpu.VMEM((rows, width), BF16),
            pltpu.VMEM((ranks, rows, width), BF16),
            pltpu.VMEM((ranks, rows, width), BF16),
            pltpu.VMEM((rows, width), BF16),
            pltpu.VMEM((rows, width), BF16),
            pltpu.SemaphoreType.DMA((8,)),
            pltpu.SemaphoreType.DMA,
            pltpu.SemaphoreType.DMA,
            pltpu.SemaphoreType.DMA((2, PIECES, 2)),
            pltpu.SemaphoreType.DMA((2, len(GROUPS))),
            pltpu.SemaphoreType.DMA((2,)),
            pltpu.SemaphoreType.DMA,
            pltpu.SemaphoreType.DMA,
        ],
        compiler_params=pltpu.CompilerParams(
            collective_id=0, has_side_effects=True, vmem_limit_bytes=40 * 1024 * 1024
        ),
        name="hstu_layer",
    )(
        *(
            pltpu.with_memory_space_constraint(array, pltpu.HBM)
            for array in (
                cand_rows.reshape(rows, width),
                listed.reshape(1, users),
                block_mask,
                hist_keys.reshape(hist, width),
                hist_values.reshape(hist, width),
                w_query.reshape(depth, width),
                w_gate.reshape(depth, width),
                w_out.reshape(depth, width),
            )
        ),
        hist_len,
    )
    return ranked.reshape(cand_rows.shape)


def solution(mesh):
    placed = (
        P("cache", None, None, "rank"),
        P(),
        P("cache"),
        P("cache", None),
        P(None, "cache", None, "rank"),
        P(None, "cache", None, "rank"),
        P(None, None, "rank"),
        P(None, None, "rank"),
        P(None, None, "rank"),
    )
    return jax.shard_map(
        functools.partial(on_device, caches=mesh.shape["cache"], ranks=mesh.shape["rank"]),
        mesh=mesh,
        in_specs=placed,
        out_specs=P("cache", None, None, "rank"),
        check_vma=False,
    )
```

```python
import functools

import jax
import jax.numpy as jnp
from jax import lax
from jax.experimental import pallas as pl
from jax.experimental.pallas import tpu as pltpu
from jax.sharding import PartitionSpec as P

BLOCK = 128
EPSILON = 1e-05
PIECES = 4
GROUPS = ((0, 1), (2,), (3,))
CHUNKS = ((0,), (1, 2))
KEY_TILE = 1024
F32 = jnp.float32
BF16 = jnp.bfloat16


def silu_of_twice(half):
    return half + half * jnp.tanh(half)


DEPTHS = 8
MESH = pl.DeviceIdType.MESH
FAR_X = (2, 1, 3, 0)


def layer_kernel(
    caches, ranks, cpr,
    cand, listed, block_mask, keys, values, w_query, w_gate, w_out, hist_len,
    ranked,
    cand_v, listed_v, mask_s, keys_v, values_v, w_in_v, w_out_v, place, send1, gathered, hidden,
    send2, recv2, load_sem, a_send, a_recv, near_recv, rest_recv, ring_send, b_send, b_recv,
):
    my_cache = lax.axis_index("cache")
    my_rank = lax.axis_index("rank")
    rows = caches * cpr
    head = keys.shape[1]
    hist = keys.shape[0]
    wide = caches // (2 * DEPTHS)
    my_core = lax.rem(my_cache, 2)
    my_z = lax.rem(my_cache // 2, DEPTHS)
    my_x = my_cache // (2 * DEPTHS)

    barrier = pltpu.get_barrier_semaphore()

    wide_part = [lax.rem(my_x + dx, wide) * (2 * DEPTHS) for dx in range(wide)]
    core_part = [my_core, 1 - my_core]

    def peer_at(dx, dz, dc):
        return wide_part[dx] + core_part[dc] + lax.rem(my_z + dz, DEPTHS) * 2

    def back(step, extent):
        return (extent - step) % extent if isinstance(step, int) else lax.rem(extent - step, extent)

    def for_depths(places, body):
        def one(step, carry):
            away = (step + 1) // 2
            dz = lax.rem(DEPTHS + DEPTHS // 2 + away * (1 - 2 * lax.rem(step, 2)), DEPTHS)
            for dx in places:
                for dc in (0, 1):
                    body(dx, dz, dc)
            return carry

        lax.fori_loop(0, DEPTHS - 1, one, 0)
        for dx in places:
            for dc in (0, 1):
                if (dx, dc) != (0, 0):
                    body(dx, 0, dc)

    def greet(dx, dz, dc):
        pl.semaphore_signal(
            barrier, inc=1, device_id=(peer_at(dx, dz, dc), my_rank), device_id_type=MESH
        )

    rank_part = [lax.rem(my_rank + step, ranks) for step in range(ranks)]

    def rank_at(step):
        return rank_part[step % ranks]

    def load(source, target, number):
        return pltpu.make_async_copy(source, target, load_sem.at[number])

    loads = [
        load(cand, cand_v, 0),
        load(listed, listed_v, 1),
        load(values, values_v, 2),
        load(block_mask, mask_s, 3),
        load(keys, keys_v, 4),
        load(w_query, w_in_v.at[:, pl.ds(0, head)], 5),
        load(w_gate, w_in_v.at[:, pl.ds(head, head)], 6),
        load(w_out, w_out_v, 7),
    ]

    for one in loads[:2]:
        one.start()
    for_depths(FAR_X, greet)
    for step in (-2, -1, 1, 2):
        pl.semaphore_signal(barrier, inc=1, device_id=(my_cache, rank_at(step)), device_id_type=MESH)
    for one in loads[2:]:
        one.start()

    users = caches
    slot_of = (
        lax.broadcasted_iota(jnp.int32, (users, rows), 1) // cpr
        == lax.broadcasted_iota(jnp.int32, (users, rows), 0)
    ).astype(F32).astype(BF16)
    loads[1].wait()
    listed_rows = jnp.broadcast_to(listed_v[...].astype(F32), (8, users)).astype(BF16)
    user_of = jnp.dot(listed_rows, slot_of, preferred_element_type=F32)[0:1, :]
    column = lax.broadcasted_iota(jnp.int32, (1, rows), 1)
    target = user_of * cpr + lax.rem(column, cpr).astype(F32)
    row_no = lax.broadcasted_iota(jnp.int32, (rows, rows), 0).astype(F32)
    moved = jnp.where(row_no == target, 1.0, 0.0)
    loads[0].wait()
    send1[...] = jnp.dot(
        moved.astype(BF16), cand_v[...], preferred_element_type=F32
    ).astype(BF16)

    pl.semaphore_wait(barrier, caches - 1 + 4)

    def of_user(user):
        return pl.ds(pl.multiple_of(user * cpr, cpr), cpr)

    def of_place(dx, dz, dc):
        return pl.ds(pl.multiple_of(((FAR_X.index(dx) * DEPTHS + dz) * 2 + dc) * cpr, cpr), cpr)

    def send_user(dx, dz, dc):
        peer = peer_at(dx, dz, dc)
        pltpu.make_async_remote_copy(
            src_ref=send1.at[of_user(peer)],
            dst_ref=gathered.at[my_rank, of_place(back(dx, wide), back(dz, DEPTHS), dc)],
            send_sem=a_send,
            recv_sem=a_recv,
            device_id=(peer, my_rank),
            device_id_type=MESH,
        ).start()

    for_depths(FAR_X, send_user)
    mine, here = of_user(my_cache), of_place(0, 0, 0)
    pltpu.make_async_copy(send1.at[mine], gathered.at[my_rank, here], a_recv).start()

    place[...] = moved.T.astype(BF16)
    for number in (2, 3):
        loads[number].wait()
    length = hist_len[0]
    for block in range(hist // BLOCK):
        events = pl.ds(block * BLOCK, BLOCK)
        limit = (length - block * BLOCK) * (mask_s[0, block] == 1).astype(jnp.int32)
        live = (lax.broadcasted_iota(jnp.int32, (BLOCK, head), 0) < limit).astype(F32)
        values_v[events, :] = (values_v[events, :].astype(F32) * live).astype(BF16)
    for number in (4, 5, 6, 7):
        loads[number].wait()
    pltpu.make_async_copy(gathered.at[my_rank], gathered.at[my_rank], a_recv).wait()

    small = rows // PIECES

    group_of = {piece: number for number, group in enumerate(GROUPS) for piece in group}

    def span_of(pieces):
        return pl.ds(pieces[0] * small, len(pieces) * small)

    def hop(buffer, phase, piece, slot, step, recv_sem):
        block = buffer.at[rank_at(slot), pl.ds(piece * small, small)]
        return pltpu.make_async_remote_copy(
            src_ref=block,
            dst_ref=block,
            send_sem=ring_send.at[phase],
            recv_sem=recv_sem,
            device_id=(my_cache, rank_at(step)),
            device_id_type=MESH,
        )

    def rest(phase, piece):
        return rest_recv.at[phase, group_of[piece]]

    def spread_near(buffer, phase, pieces):
        for piece in pieces:
            for way, step in ((0, 2), (1, -2)):
                hop(buffer, phase, piece, 0, step, near_recv.at[phase, piece, way]).start()

    def spread_next(buffer, phase, pieces):
        for piece in pieces:
            for step in (1, -1):
                hop(buffer, phase, piece, 0, step, rest(phase, piece)).start()

    def relay(buffer, phase, pieces):
        for piece in pieces:
            for way, step in ((0, 1), (1, -1)):
                hop(buffer, phase, piece, -2 * step, 2 * step, near_recv.at[phase, piece, way]).wait_recv()
                if piece % 2 == way:
                    hop(buffer, phase, piece, -2 * step, 2 * step, rest(phase, piece)).start()
                hop(buffer, phase, piece, -2 * step, step, rest(phase, piece)).start()

    def complete(buffer, phase, group):
        five = buffer.at[pl.ds(0, 5), span_of(GROUPS[group])]
        pltpu.make_async_copy(five, five, rest_recv.at[phase, group]).wait()

    def exchange(buffer, phase):
        every = range(PIECES)
        spread_next(buffer, phase, every[:-1])
        relay(buffer, phase, every)
        spread_next(buffer, phase, every[-1:])

    def pieces_of(chunk):
        return [piece for group in chunk for piece in GROUPS[group]]

    spread_near(gathered, 0, range(PIECES))
    exchange(gathered, 0)

    for chunk in CHUNKS:
        for group in chunk:
            complete(gathered, 0, group)
        span = span_of(pieces_of(chunk))
        slices = [gathered[k, span, :].astype(F32) for k in range(ranks)]
        centre = jnp.sum(sum(slices[1:], slices[0]), axis=-1, keepdims=True) * (1.0 / (ranks * head))
        slices = [s - centre for s in slices]
        squares = [s * s for s in slices]
        spread_of = jnp.sum(sum(squares[1:], squares[0]), axis=-1, keepdims=True) * (1.0 / (ranks * head))
        factor = lax.rsqrt(spread_of + EPSILON)
        normed = jnp.concatenate([(s * factor).astype(BF16) for s in slices], axis=1)
        both = silu_of_twice(0.5 * jnp.dot(normed, w_in_v[...], preferred_element_type=F32))
        queries = both[:, :head].astype(BF16)
        gate = both[:, head:]
        attended = jnp.zeros((span.size, head), F32)
        for tile in range(hist // KEY_TILE):
            events = pl.ds(tile * KEY_TILE, KEY_TILE)
            scores = lax.dot_general(
                queries, keys_v[events, :], (((1,), (1,)), ((), ())), preferred_element_type=F32
            )
            weights = silu_of_twice(scores * (0.5 * head ** -0.5)).astype(BF16)
            attended += jnp.dot(weights, values_v[events, :], preferred_element_type=F32)
        centre = jnp.mean(attended, axis=-1, keepdims=True)
        attended = attended - centre
        spread_of = jnp.mean(attended * attended, axis=-1, keepdims=True)
        hidden[my_rank, span, :] = (attended * lax.rsqrt(spread_of + EPSILON) * gate).astype(BF16)
        spread_near(hidden, 1, pieces_of(chunk))

    exchange(hidden, 1)

    for group, pieces in enumerate(GROUPS):
        complete(hidden, 1, group)
        span = span_of(pieces)
        whole = jnp.concatenate([hidden[k, span, :] for k in range(ranks)], axis=1)
        projected = jnp.dot(whole, w_out_v[...], preferred_element_type=F32)
        send2[span, :] = (gathered[my_rank, span, :].astype(F32) + projected).astype(BF16)

        def send_shard(dx, dz, dc):
            pltpu.make_async_remote_copy(
                src_ref=send2.at[of_place(dx, dz, dc)],
                dst_ref=recv2.at[mine],
                send_sem=b_send,
                recv_sem=b_recv,
                device_id=(peer_at(dx, dz, dc), my_rank),
                device_id_type=MESH,
            ).start()

        for_depths([FAR_X[piece] for piece in pieces], send_shard)
    pltpu.make_async_copy(send2.at[here], recv2.at[mine], b_recv).start()

    pltpu.make_async_copy(recv2, recv2, b_recv).wait()
    ranked[...] = jnp.dot(place[...], recv2[...], preferred_element_type=F32).astype(BF16)

    others = pl.ds(0, rows - cpr)
    pltpu.make_async_copy(send1.at[others], send1.at[others], a_send).wait()
    pltpu.make_async_copy(send2.at[others], send2.at[others], b_send).wait()
    for phase, buffer in ((0, gathered), (1, hidden)):
        seven = buffer.at[pl.ds(0, ranks - 1)]
        pltpu.make_async_copy(seven, seven, ring_send.at[phase]).wait()


def on_device(
    cand_rows, listed, hist_len, block_mask, hist_keys, hist_values, w_query, w_gate, w_out, *, caches, ranks
):
    _, users, cpr, width = cand_rows.shape
    rows = users * cpr
    hist = hist_keys.shape[2]
    depth = w_query.shape[1]
    in_hbm = pl.BlockSpec(memory_space=pltpu.HBM)
    vmem = pl.BlockSpec(memory_space=pltpu.VMEM)
    ranked = pl.pallas_call(
        functools.partial(layer_kernel, caches, ranks, cpr),
        out_shape=jax.ShapeDtypeStruct((rows, width), BF16),
        in_specs=[in_hbm] * 8 + [pl.BlockSpec(memory_space=pltpu.SMEM)],
        out_specs=vmem,
        scratch_shapes=[
            pltpu.VMEM((rows, width), BF16),
            pltpu.VMEM((1, users), jnp.int32),
            pltpu.SMEM(block_mask.shape, jnp.int32),
            pltpu.VMEM((hist, width), BF16),
            pltpu.VMEM((hist, width), BF16),
            pltpu.VMEM((depth, 2 * width), BF16),
            pltpu.VMEM((depth, width), BF16),
            pltpu.VMEM((rows, rows), BF16),
            pltpu.VMEM((rows, width), BF16),
            pltpu.VMEM((ranks, rows, width), BF16),
            pltpu.VMEM((ranks, rows, width), BF16),
            pltpu.VMEM((rows, width), BF16),
            pltpu.VMEM((rows, width), BF16),
            pltpu.SemaphoreType.DMA((8,)),
            pltpu.SemaphoreType.DMA,
            pltpu.SemaphoreType.DMA,
            pltpu.SemaphoreType.DMA((2, PIECES, 2)),
            pltpu.SemaphoreType.DMA((2, len(GROUPS))),
            pltpu.SemaphoreType.DMA((2,)),
            pltpu.SemaphoreType.DMA,
            pltpu.SemaphoreType.DMA,
        ],
        compiler_params=pltpu.CompilerParams(
            collective_id=0, has_side_effects=True, vmem_limit_bytes=40 * 1024 * 1024
        ),
        name="hstu_layer",
    )(
        *(
            pltpu.with_memory_space_constraint(array, pltpu.HBM)
            for array in (
                cand_rows.reshape(rows, width),
                listed.reshape(1, users),
                block_mask,
                hist_keys.reshape(hist, width),
                hist_values.reshape(hist, width),
                w_query.reshape(depth, width),
                w_gate.reshape(depth, width),
                w_out.reshape(depth, width),
            )
        ),
        hist_len,
    )
    return ranked.reshape(cand_rows.shape)


def solution(mesh):
    placed = (
        P("cache", None, None, "rank"),
        P(),
        P("cache"),
        P("cache", None),
        P(None, "cache", None, "rank"),
        P(None, "cache", None, "rank"),
        P(None, None, "rank"),
        P(None, None, "rank"),
        P(None, None, "rank"),
    )
    return jax.shard_map(
        functools.partial(on_device, caches=mesh.shape["cache"], ranks=mesh.shape["rank"]),
        mesh=mesh,
        in_specs=placed,
        out_specs=P("cache", None, None, "rank"),
        check_vma=False,
    )
```
